32 devices in a mesh: ctx: 8 (over y, x, core), head: 4 (over z).
Axes of the slice: x: 2, y: 2, z: 4, core: 2. Of those that a mesh axis runs over, the one named last changes fastest.
Arguments:
- query_noisy: bfloat16 [4096, 2048], P(('ctx', 'head')), may hold values from -7 to 7
- key_noisy: bfloat16 [4096, 2048], P(('ctx', 'head')), may hold values from -7 to 7
- value_noisy: bfloat16 [4096, 2048], P(('ctx', 'head')), may hold values from -48 to 48
- key_clean: bfloat16 [4096, 2048], P(('ctx', 'head')), may hold values from -6 to 6
- value_clean: bfloat16 [4096, 2048], P(('ctx', 'head')), may hold values from -48 to 48
- grad_output: bfloat16 [4096, 2048], P(('ctx', 'head')), may hold values from -192 to 192
- block_list: int32 [16, 4], replicated, may hold values from -1 to 14, as said below
Outputs:
- attended: bfloat16 [4096, 2048], P(('ctx', 'head'))
- query_grad: bfloat16 [4096, 2048], P(('ctx', 'head'))
- noisykey_grad: bfloat16 [4096, 2048], P(('ctx', 'head'))
- noisyvalue_grad: bfloat16 [4096, 2048], P(('ctx', 'head'))
- cleankey_grad: bfloat16 [4096, 2048], P(('ctx', 'head'))
- cleanvalue_grad: bfloat16 [4096, 2048], P(('ctx', 'head'))
The draws below stay inside these ranges and needn't reach their ends.
Inputs may be any that keep to these rules, and one draw needn't show every extreme that they name: `block_list`: each entry of row b is -1 or a block before b. The 8 entries in the rows of one index of ctx name blocks of any one index of ctx at most 1 times, and that most is reached in every draw. The first entry of the first row of every index of ctx after the first names a block of index 0. The last entry of each index's last row names that index's block 0.
All inputs are finite; a program needn't handle non-finite values.
Results may differ from the reference program's by a relative error of at most 0.03.
Values may be sent and summed in bfloat16 or wider, within the bound.
No kernel may reach another device: no remote copies, remote signals or barrier semaphores. Data moves between devices by JAX's collectives and lax.ppermute only.
A program may use at most 128 MiB of HBM per device.

```python
import math
import jax
import jax.numpy as jnp
from jax import lax

HD = 128
HEADS = 16
BLK = 256
SEL = 4
BLK_DEV = 2
NBLK = 16
TOKENS = 4096


def base_values(key):
    shape = (NBLK * BLK, HEADS * HD)
    return jnp.clip(jax.random.normal(key, shape, jnp.float32), -6.0, 6.0)


def draw_query_noisy(key, part):
    values = base_values(jax.random.fold_in(key, 1))
    return values.astype(jnp.bfloat16)


def draw_key_noisy(key, part):
    values = base_values(jax.random.fold_in(key, 2))
    return values.astype(jnp.bfloat16)


def draw_block_list(key, part):
    devices = NBLK // BLK_DEV
    requests = BLK_DEV * SEL
    capacity = -(-requests // devices)
    candidates = jnp.repeat(jnp.arange(devices, dtype=jnp.int32), capacity)

    def one_device(index):
        sub_key = jax.random.fold_in(key, index)
        shuffled = jax.random.permutation(jax.random.fold_in(sub_key, 1), devices * capacity)
        owners = candidates[shuffled]
        usable = owners < index
        order_key = jnp.where(usable & (owners == 0), 0, jnp.where(usable, 1, 2)).astype(jnp.int32)
        arranged = owners[jnp.argsort(order_key, stable=True)][:requests - 1]
        local_pick = jax.random.randint(jax.random.fold_in(sub_key, 2), (requests - 1,), 0, BLK_DEV)
        listed = jnp.where(arranged < index, arranged * BLK_DEV + local_pick, -1)
        own_entry = index * BLK_DEV + BLK_DEV - 2
        return jnp.concatenate([listed, own_entry[None]]).astype(jnp.int32)
    all_lists = jax.vmap(one_device)(jnp.arange(devices, dtype=jnp.int32))
    return all_lists.reshape(NBLK, SEL)


def block_levels(own_key, dims, cuts, least, largest):
    gain, own = 1.0, jax.random.fold_in(own_key, 6)
    for axis_at, parts in cuts:
        steps = jnp.exp(jax.random.uniform(jax.random.fold_in(own, axis_at), (parts,), jnp.float32, least / len(cuts), largest / len(cuts)))
        gain = gain * jnp.repeat(steps, dims[axis_at] // parts).reshape([-1 if axis == axis_at else 1 for axis in range(len(dims))])
    return gain


def gaussian(rng, shape, spread, reach, shards=(), kind=jnp.bfloat16):
    loudness = block_levels(rng, shape, shards, -0.22, 0.18) if shards else 1.0
    drawn = jax.random.normal(rng, shape, jnp.float32) * spread * loudness
    return jnp.minimum(jnp.maximum(drawn, -reach), reach).astype(kind)


def setup_inputs(seed: int = 0) -> dict:
    streams_of = jax.random.split(jax.random.key(seed), 8)
    return {
        "query_noisy": draw_query_noisy(jax.random.fold_in(streams_of[7], 71), 0),
        "key_noisy": draw_key_noisy(jax.random.fold_in(streams_of[7], 71), 0),
        "value_noisy": gaussian(streams_of[2], (TOKENS, HEADS * HD), 8.0, 48.0, ((0, 32),)),
        "key_clean": gaussian(streams_of[3], (TOKENS, HEADS * HD), 1.0, 6.0, ((0, 32),)),
        "value_clean": gaussian(streams_of[4], (TOKENS, HEADS * HD), 8.0, 48.0, ((0, 32),)),
        "grad_output": gaussian(streams_of[5], (TOKENS, HEADS * HD), 32.0, 192.0, ((0, 32),)),
        "block_list": draw_block_list(jax.random.fold_in(streams_of[7], 71), 0),
    }


masked_value = -1e+30

def to_blocks(array):
    return array.reshape(NBLK, BLK, HEADS, HD).transpose(0, 2, 1, 3)

def to_rows(array):
    return array.transpose(0, 2, 1, 3).reshape(TOKENS, HEADS * HD)

def reference(query_noisy, key_noisy, value_noisy, key_clean, value_clean, grad_output, block_list):
    score_scale = 1.0 / math.sqrt(HD)
    query_blocks = to_blocks(query_noisy)
    key_blocks = to_blocks(key_noisy)
    value_blocks = to_blocks(value_noisy)
    clean_keys = to_blocks(key_clean)
    clean_values = to_blocks(value_clean)
    grad_blocks = to_blocks(grad_output)
    key_total = (1 + SEL) * BLK

    def one_block(carry, inputs):
        kgrad_sum, vgrad_sum = carry
        query_block, key_block, value_block, grad_block, entries = inputs
        is_valid = entries >= 0
        index = jnp.where(is_valid, entries, 0).astype(jnp.int32)
        all_keys = jnp.concatenate([key_block[None], clean_keys[index]], 0).transpose(1, 0, 2, 3).reshape(HEADS, key_total, HD)
        all_values = jnp.concatenate([value_block[None], clean_values[index]], 0).transpose(1, 0, 2, 3).reshape(HEADS, key_total, HD)
        live_keys = jnp.repeat(jnp.concatenate([jnp.ones((1,), bool), is_valid]), BLK)
        query32 = query_block.astype(jnp.float32)
        keys32 = all_keys.astype(jnp.float32)
        values32 = all_values.astype(jnp.float32)
        grad32 = grad_block.astype(jnp.float32)
        scores = jnp.einsum('hqd,hkd->hqk', query32, keys32) * score_scale
        scores = jnp.where(live_keys, scores, masked_value)
        row_max = lax.optimization_barrier(jnp.max(scores, -1, keepdims=True))
        log_total = row_max + jnp.log(lax.optimization_barrier(jnp.sum(jnp.exp(scores - row_max), -1, keepdims=True)))
        prob = jnp.where(live_keys, jnp.exp(scores - log_total), 0.0)
        prob_bf = prob.astype(jnp.bfloat16)
        prob_back = prob_bf.astype(jnp.float32)
        attended = jnp.einsum('hqk,hkd->hqd', prob_back, values32).astype(jnp.bfloat16)
        row_delta = lax.optimization_barrier(jnp.sum(grad32 * attended.astype(jnp.float32), -1, keepdims=True))
        dprob = jnp.einsum('hqd,hkd->hqk', grad32, values32)
        dscore = prob * (dprob - row_delta)
        dscore_back = dscore.astype(jnp.bfloat16).astype(jnp.float32)
        query_grad = (jnp.einsum('hqk,hkd->hqd', dscore_back, keys32) * score_scale).astype(jnp.bfloat16)
        kterm = jnp.einsum('hqk,hqd->hkd', dscore_back, query32) * score_scale
        vterm = jnp.einsum('hqk,hqd->hkd', prob_back, grad32)
        key_self = kterm[:, :BLK].astype(jnp.bfloat16)
        value_self = vterm[:, :BLK].astype(jnp.bfloat16)
        live_float = is_valid.astype(jnp.float32)[:, None, None, None]
        ktiles = kterm[:, BLK:].reshape(HEADS, SEL, BLK, HD).transpose(1, 0, 2, 3)
        vtiles = vterm[:, BLK:].reshape(HEADS, SEL, BLK, HD).transpose(1, 0, 2, 3)
        ktiles = lax.optimization_barrier(ktiles.astype(jnp.bfloat16)).astype(jnp.float32) * live_float
        vtiles = lax.optimization_barrier(vtiles.astype(jnp.bfloat16)).astype(jnp.float32) * live_float
        kgrad_sum = kgrad_sum.at[index].add(ktiles)
        vgrad_sum = vgrad_sum.at[index].add(vtiles)
        return ((kgrad_sum, vgrad_sum), (attended, query_grad, key_self, value_self))
    start = (jnp.zeros((NBLK, HEADS, BLK, HD), jnp.float32), jnp.zeros((NBLK, HEADS, BLK, HD), jnp.float32))
    (kgrad_sum, vgrad_sum), stacked = lax.scan(one_block, start, (query_blocks, key_blocks, value_blocks, grad_blocks, block_list))
    attended, query_grad, key_self, value_self = stacked
    return (to_rows(attended), to_rows(query_grad), to_rows(key_self), to_rows(value_self), to_rows(kgrad_sum.astype(jnp.bfloat16)), to_rows(vgrad_sum.astype(jnp.bfloat16)))
```

```python
import functools
import math

import jax
import jax.numpy as jnp
from jax import lax
from jax.experimental import pallas as pl
from jax.experimental.pallas import tpu as pltpu
from jax.sharding import PartitionSpec as P

HD = 128
BLK = 256
SEL = 4
CHUNKS = 1

MASKED = -1e30
BF = jnp.bfloat16
F32 = jnp.float32


HBM = pl.BlockSpec(memory_space=pl.ANY)
SMEM = pl.BlockSpec(memory_space=pltpu.SMEM)


def cost(nbytes, flops=0, trans=0):
    return pl.CostEstimate(flops=flops, bytes_accessed=nbytes, transcendentals=trans)


def swap(x, axis, mask):
    count = lax.axis_size(axis)
    return lax.ppermute(x, axis, [(i, i ^ mask) for i in range(count)])


class Plan:
    def __init__(self, rows, features, blocks, chunks):
        self.ctx = lax.axis_size("ctx")
        self.n = lax.axis_size("head")
        self.rows = rows
        self.features = features
        self.bh = blocks // self.ctx
        self.per = self.n // self.bh
        self.group = features // self.n
        self.heads = self.group // HD
        self.chunks = min(chunks, self.heads)
        self.width = self.group // self.chunks
        self.tile = (2, self.per, rows, self.width)
        self.tile_bytes = 2 * BLK * self.width * 2

    def cols(self, z, mask, chunk):
        start = (z ^ mask) * self.group + chunk * self.width
        return pl.ds(pl.multiple_of(start, HD), self.width)


def run_all(copies):
    for c in copies:
        c.start()
    return copies


def wait_all(copies):
    for c in copies:
        c.wait()


def pack(plan, arrays, chunk):
    k, n = len(arrays), plan.n

    def body(*refs):
        ins, outs = refs[:k], refs[k : k + n - 1]
        buf, sem_in, sem_out = refs[k + n - 1 :]
        z = lax.axis_index("head")
        loads = [
            run_all(
                [
                    pltpu.make_async_copy(
                        ins[i].at[:, plan.cols(z, m, chunk)],
                        buf.at[m - 1, i],
                        sem_in.at[m - 1, i],
                    )
                    for i in range(k)
                ]
            )
            for m in range(1, n)
        ]
        stores = []
        for m in range(1, n):
            wait_all(loads[m - 1])
            stores += run_all(
                [pltpu.make_async_copy(buf.at[m - 1], outs[m - 1], sem_out.at[m - 1])]
            )
        wait_all(stores)

    shape = (k, plan.rows, plan.width)
    return pl.pallas_call(
        body,
        out_shape=[jax.ShapeDtypeStruct(shape, BF)] * (n - 1),
        in_specs=[HBM] * k,
        out_specs=[HBM] * (n - 1),
        scratch_shapes=[
            pltpu.VMEM((n - 1,) + shape, BF),
            pltpu.SemaphoreType.DMA((n - 1, k)),
            pltpu.SemaphoreType.DMA((n - 1,)),
        ],
        cost_estimate=cost(2 * k * (n - 1) * plan.rows * plan.width * 2),
        name="pack",
    )(*arrays)


def unpack(plan, pieces, k):
    n, chunks = plan.n, plan.chunks
    flat = [p for chunk in pieces for p in chunk]

    def body(*refs):
        ins, outs = refs[: n * chunks], refs[n * chunks : n * chunks + k]
        buf, sem_in, sem_out = refs[n * chunks + k :]
        z = lax.axis_index("head")
        loads = []
        for c in range(chunks):
            for m in range(n):
                at = c * n + m
                loads.append(
                    pltpu.make_async_copy(
                        ins[at], buf.at[:, :, plan.cols(z, m, c)], sem_in.at[at]
                    )
                )
        run_all(loads)
        wait_all(loads)
        wait_all(
            run_all([pltpu.make_async_copy(buf.at[i], outs[i], sem_out.at[i]) for i in range(k)])
        )

    shape = (plan.rows, plan.features)
    return pl.pallas_call(
        body,
        out_shape=[jax.ShapeDtypeStruct(shape, BF)] * k,
        in_specs=[HBM] * len(flat),
        out_specs=[HBM] * k,
        scratch_shapes=[
            pltpu.VMEM((k,) + shape, BF),
            pltpu.SemaphoreType.DMA((len(flat),)),
            pltpu.SemaphoreType.DMA((k,)),
        ],
        cost_estimate=cost(2 * k * plan.rows * plan.features * 2),
        name="unpack",
    )(*flat)


def wanted(plan, lists, reader, owner, z):
    live, which = jnp.int32(0), jnp.int32(0)
    for e in range(plan.bh * SEL):
        entry = lists[reader * plan.bh + e // SEL, e % SEL]
        hit = (entry >= 0) & (lax.div(entry, jnp.int32(plan.bh)) == owner)
        local = lax.rem(entry, jnp.int32(plan.bh)) ^ lax.div(z, jnp.int32(plan.per))
        live = jnp.where(hit, 1, live)
        which = jnp.where(hit, local, which)
    return live, which


def select(plan, kclean, vclean, got, lists, chunk):
    n, per, slots = plan.n, plan.per, plan.ctx

    def body(*refs):
        lists_ref, k_ref, v_ref = refs[:3]
        ins, outs = refs[3 : 2 + n], refs[2 + n : 2 + n + slots]
        buf, sem_own, sem_in, sem_out = refs[2 + n + slots :]
        me, z = lax.axis_index("ctx"), lax.axis_index("head")
        own = plan.cols(z, 0, chunk)
        loads = [
            pltpu.make_async_copy(k_ref.at[:, own], buf.at[0, 0, 0], sem_own.at[0]),
            pltpu.make_async_copy(v_ref.at[:, own], buf.at[0, 1, 0], sem_own.at[1]),
        ]
        for m in range(1, n):
            loads.append(
                pltpu.make_async_copy(
                    ins[m - 1], buf.at[m // per, :, m % per], sem_in.at[m - 1]
                )
            )
        run_all(loads)
        choice = [wanted(plan, lists_ref, me ^ s, me, z)[1] for s in range(slots)]
        wait_all(loads)
        wait_all(
            run_all(
                [
                    pltpu.make_async_copy(buf.at[choice[s]], outs[s], sem_out.at[s])
                    for s in range(slots)
                ]
            )
        )

    return pl.pallas_call(
        body,
        out_shape=[jax.ShapeDtypeStruct(plan.tile, BF)] * slots,
        in_specs=[SMEM] + [HBM] * (n + 1),
        out_specs=[HBM] * slots,
        scratch_shapes=[
            pltpu.VMEM((plan.bh,) + plan.tile, BF),
            pltpu.SemaphoreType.DMA((2,)),
            pltpu.SemaphoreType.DMA((n - 1,)),
            pltpu.SemaphoreType.DMA((slots,)),
        ],
        cost_estimate=cost((slots + plan.bh) * plan.tile_bytes),
        name="select",
    )(lists, kclean, vclean, *got)


def dot(a, b, ca, cb):
    return lax.dot_general(a, b, (((ca,), (cb,)), ((), ())), preferred_element_type=F32)


def attend(plan, noisy, got, tiles, lists, chunk):
    n, per, slots, rows, bh = plan.n, plan.per, plan.ctx, plan.rows, plan.bh
    heads = plan.width // HD
    scale = 1.0 / math.sqrt(HD)
    log2e = 1.0 / math.log(2.0)
    side = (4, rows, plan.width)

    def body(*refs):
        at = 0

        def take(count):
            nonlocal at
            at += count
            return refs[at - count : at]

        (lists_ref,) = take(1)
        own_refs = take(4)
        got_refs = take(n - 1)
        tile_refs = take(slots)
        side_refs = take(n)
        term_refs = take(slots)
        rows_in, tiles_in, rows_out, terms_out, sem_own, sem_got, sem_tile, sem_side, sem_term = (
            refs[at:]
        )
        me, z = lax.axis_index("ctx"), lax.axis_index("head")
        home = lax.div(z, jnp.int32(per))
        own = plan.cols(z, 0, chunk)
        loads = [
            pltpu.make_async_copy(own_refs[i].at[:, own], rows_in.at[i, 0, 0], sem_own.at[i])
            for i in range(4)
        ]
        loads += [
            pltpu.make_async_copy(
                got_refs[m - 1], rows_in.at[:, m // per, m % per], sem_got.at[m - 1]
            )
            for m in range(1, n)
        ]
        loads += [
            pltpu.make_async_copy(tile_refs[s], tiles_in.at[s], sem_tile.at[s])
            for s in range(slots)
        ]
        run_all(loads)
        wait_all(loads)

        def step(i, carry):
            h, b = lax.div(i, jnp.int32(bh)), lax.rem(i, jnp.int32(bh))
            cols = pl.ds(pl.multiple_of(h * HD, HD), HD)

            def block(ref, *index):
                return ref[(*index, slice(None), slice(None), cols)].reshape(BLK, HD)

            def put(ref, value, *index):
                ref[(*index, slice(None), slice(None), cols)] = value.astype(BF).reshape(
                    per, rows, HD
                )

            q, k0, v0, g = (block(rows_in, j, b) for j in range(4))
            row = me * bh + (b ^ home)
            keys, values, bias, target = [k0], [v0], [None], []
            for s in range(SEL):
                entry = lists_ref[row, s]
                live = entry >= 0
                slot = jnp.where(live, lax.div(entry, jnp.int32(bh)) ^ me, 0)
                keys.append(block(tiles_in, slot, 0))
                values.append(block(tiles_in, slot, 1))
                bias.append(jnp.where(live, 0.0, MASKED).astype(F32))
                target.append(jnp.where(live, slot, slots))
            scores = []
            for kt, extra in zip(keys, bias):
                s = dot(kt, q, 1, 1) * (scale * log2e)
                scores.append(s if extra is None else s + extra)
            top = functools.reduce(
                jnp.maximum, [jnp.max(s, axis=0, keepdims=True) for s in scores]
            )
            weights = [jnp.exp2(s - top) for s in scores]
            total = functools.reduce(
                jnp.add, [jnp.sum(w, axis=0, keepdims=True) for w in weights]
            )
            inverse = 1.0 / total
            probs = [w * inverse for w in weights]
            probs_bf = [p.astype(BF) for p in probs]
            out_t = functools.reduce(
                jnp.add, [dot(vt.T, p, 1, 0) for vt, p in zip(values, probs_bf)]
            )
            out_bf = out_t.astype(BF)
            put(rows_out, out_bf.T, 0, b)
            delta = jnp.sum(g.T.astype(F32) * out_bf.astype(F32), axis=0, keepdims=True)
            dq_t = jnp.zeros((HD, BLK), F32)
            for t in range(1 + SEL):
                ds = (probs[t] * (dot(values[t], g, 1, 1) - delta)).astype(BF)
                dq_t = dq_t + dot(keys[t].T, ds, 1, 0)
                kterm = dot(ds, q, 1, 0) * scale
                vterm = dot(probs_bf[t], g, 1, 0)
                if t == 0:
                    put(rows_out, kterm, 2, b)
                    put(rows_out, vterm, 3, b)
                else:
                    put(terms_out, kterm, target[t - 1], 0)
                    put(terms_out, vterm, target[t - 1], 1)
            put(rows_out, (dq_t * scale).astype(BF).T, 1, b)
            return carry

        lax.fori_loop(0, heads * bh, step, 0)
        stores = [
            pltpu.make_async_copy(terms_out.at[s], term_refs[s], sem_term.at[s])
            for s in range(slots)
        ]
        stores += [
            pltpu.make_async_copy(rows_out.at[:, m // per, m % per], side_refs[m], sem_side.at[m])
            for m in range(n)
        ]
        run_all(stores)
        wait_all(stores)

    flops = heads * bh * 6 * 2 * BLK * (1 + SEL) * BLK * HD
    result = pl.pallas_call(
        body,
        out_shape=[jax.ShapeDtypeStruct(side, BF)] * n
        + [jax.ShapeDtypeStruct(plan.tile, BF)] * slots,
        in_specs=[SMEM] + [HBM] * (4 + n - 1 + slots),
        out_specs=[HBM] * (n + slots),
        scratch_shapes=[
            pltpu.VMEM((4, bh, per, rows, plan.width), BF),
            pltpu.VMEM((slots,) + plan.tile, BF),
            pltpu.VMEM((4, bh, per, rows, plan.width), BF),
            pltpu.VMEM((slots + 1,) + plan.tile, BF),
            pltpu.SemaphoreType.DMA((4,)),
            pltpu.SemaphoreType.DMA((n - 1,)),
            pltpu.SemaphoreType.DMA((slots,)),
            pltpu.SemaphoreType.DMA((n,)),
            pltpu.SemaphoreType.DMA((slots,)),
        ],
        compiler_params=pltpu.CompilerParams(vmem_limit_bytes=48 * 1024 * 1024),
        cost_estimate=cost(
            2 * (slots * plan.tile_bytes + 4 * bh * BLK * plan.width * 2),
            flops,
            heads * bh * BLK * (1 + SEL) * BLK,
        ),
        name="attend",
    )(lists, *noisy, *got, *tiles)
    return result[:n], result[n:]


def total_terms(plan, terms, lists):
    n, per, slots, rows, bh = plan.n, plan.per, plan.ctx, plan.rows, plan.bh

    def body(*refs):
        lists_ref, ins, outs = refs[0], refs[1 : 1 + slots], refs[1 + slots : 1 + slots + n]
        buf, summed, sem_in, sem_out = refs[1 + slots + n :]
        me, z = lax.axis_index("ctx"), lax.axis_index("head")
        loads = run_all(
            [pltpu.make_async_copy(ins[s], buf.at[s], sem_in.at[s]) for s in range(slots)]
        )
        asked = [wanted(plan, lists_ref, me ^ s, me, z) for s in range(slots)]
        wait_all(loads)
        stripe = math.gcd(rows, 32)

        def step(i, carry):
            at = pl.ds(pl.multiple_of(i * stripe, stripe), stripe)
            for kv in range(2):
                for p in range(per):
                    parts = [buf[s, kv, p, at, :].astype(F32) for s in range(slots)]
                    for j in range(bh):
                        acc = jnp.zeros((stripe, plan.width), F32)
                        for (live, which), part in zip(asked, parts):
                            acc = acc + jnp.where((live > 0) & (which == j), part, 0.0)
                        summed[j, kv, p, at, :] = acc.astype(BF)
            return carry

        lax.fori_loop(0, rows // stripe, step, 0)
        wait_all(
            run_all(
                [
                    pltpu.make_async_copy(summed.at[m // per, :, m % per], outs[m], sem_out.at[m])
                    for m in range(n)
                ]
            )
        )

    shape = (2, rows, plan.width)
    return pl.pallas_call(
        body,
        out_shape=[jax.ShapeDtypeStruct(shape, BF)] * n,
        in_specs=[SMEM] + [HBM] * slots,
        out_specs=[HBM] * n,
        scratch_shapes=[
            pltpu.VMEM((slots,) + plan.tile, BF),
            pltpu.VMEM((bh,) + plan.tile, BF),
            pltpu.SemaphoreType.DMA((slots,)),
            pltpu.SemaphoreType.DMA((n,)),
        ],
        cost_estimate=cost((slots + bh) * plan.tile_bytes),
        name="total_terms",
    )(lists, *terms)


def slot_order(slots):
    return sorted(range(1, slots), key=lambda s: (-bin(s >> 1).count("1"), s >> 1 == 0, s))


def over_head(parts):
    got = {m: swap(parts[m - 1], "head", m) for m in range(len(parts), 0, -1)}
    return [got[m] for m in range(1, len(parts) + 1)]


def over_ctx(parts):
    got = {s: swap(parts[s], "ctx", s) for s in slot_order(len(parts))}
    return [parts[0]] + [got[s] for s in range(1, len(parts))]


def shards(query, key, value, kclean, vclean, grad, lists):
    plan = Plan(query.shape[0], query.shape[1], lists.shape[0], CHUNKS)
    noisy = (query, key, value, grad)
    sides, cleans = [], []
    for c in range(plan.chunks):
        got_clean = over_head(pack(plan, (kclean, vclean), c))
        got_noisy = over_head(pack(plan, noisy, c))
        tiles = over_ctx(select(plan, kclean, vclean, got_clean, lists, c))
        side, terms = attend(plan, noisy, got_noisy, tiles, lists, c)
        sides.append([side[0]] + over_head(side[1:]))
        clean = total_terms(plan, over_ctx(terms), lists)
        cleans.append([clean[0]] + over_head(clean[1:]))
    return (*unpack(plan, sides, 4), *unpack(plan, cleans, 2))


def solution(mesh):
    rows = P(("ctx", "head"), None)
    return jax.shard_map(
        shards,
        mesh=mesh,
        in_specs=(rows,) * 6 + (P(),),
        out_specs=(rows,) * 6,
        check_vma=False,
    )
```

```python
import functools
import math

import jax
import jax.numpy as jnp
from jax import lax
from jax.experimental import pallas as pl
from jax.experimental.pallas import tpu as pltpu
from jax.sharding import PartitionSpec as P

HD = 128
BLK = 256
SEL = 4
CHUNKS = 2

MASKED = -1e30
BF = jnp.bfloat16
F32 = jnp.float32


HBM = pl.BlockSpec(memory_space=pl.ANY)
SMEM = pl.BlockSpec(memory_space=pltpu.SMEM)


def cost(nbytes, flops=0, trans=0):
    return pl.CostEstimate(flops=flops, bytes_accessed=nbytes, transcendentals=trans)


def swap(x, axis, mask):
    count = lax.axis_size(axis)
    return lax.ppermute(x, axis, [(i, i ^ mask) for i in range(count)])


class Plan:
    def __init__(self, rows, features, blocks, chunks):
        self.ctx = lax.axis_size("ctx")
        self.n = lax.axis_size("head")
        self.rows = rows
        self.features = features
        self.bh = blocks // self.ctx
        self.per = self.n // self.bh
        self.group = features // self.n
        self.heads = self.group // HD
        self.chunks = min(chunks, self.heads)
        self.width = self.group // self.chunks
        self.tile = (2, self.per, rows, self.width)
        self.tile_bytes = 2 * BLK * self.width * 2

    def cols(self, z, mask, chunk):
        start = (z ^ mask) * self.group + chunk * self.width
        return pl.ds(pl.multiple_of(start, HD), self.width)


def run_all(copies):
    for c in copies:
        c.start()
    return copies


def wait_all(copies):
    for c in copies:
        c.wait()


def pack(plan, arrays, chunk):
    k, n = len(arrays), plan.n

    def body(*refs):
        ins, outs = refs[:k], refs[k : k + n - 1]
        buf, sem_in, sem_out = refs[k + n - 1 :]
        z = lax.axis_index("head")
        loads = [
            run_all(
                [
                    pltpu.make_async_copy(
                        ins[i].at[:, plan.cols(z, m, chunk)],
                        buf.at[m - 1, i],
                        sem_in.at[m - 1, i],
                    )
                    for i in range(k)
                ]
            )
            for m in range(1, n)
        ]
        stores = []
        for m in range(1, n):
            wait_all(loads[m - 1])
            stores += run_all(
                [pltpu.make_async_copy(buf.at[m - 1], outs[m - 1], sem_out.at[m - 1])]
            )
        wait_all(stores)

    shape = (k, plan.rows, plan.width)
    return pl.pallas_call(
        body,
        out_shape=[jax.ShapeDtypeStruct(shape, BF)] * (n - 1),
        in_specs=[HBM] * k,
        out_specs=[HBM] * (n - 1),
        scratch_shapes=[
            pltpu.VMEM((n - 1,) + shape, BF),
            pltpu.SemaphoreType.DMA((n - 1, k)),
            pltpu.SemaphoreType.DMA((n - 1,)),
        ],
        cost_estimate=cost(2 * k * (n - 1) * plan.rows * plan.width * 2),
        name="pack",
    )(*arrays)


def unpack(plan, pieces, k):
    n, chunks = plan.n, plan.chunks
    flat = [p for chunk in pieces for p in chunk]

    def body(*refs):
        ins, outs = refs[: n * chunks], refs[n * chunks : n * chunks + k]
        buf, sem_in, sem_out = refs[n * chunks + k :]
        z = lax.axis_index("head")
        loads = []
        for c in range(chunks):
            for m in range(n):
                at = c * n + m
                loads.append(
                    pltpu.make_async_copy(
                        ins[at], buf.at[:, :, plan.cols(z, m, c)], sem_in.at[at]
                    )
                )
        run_all(loads)
        wait_all(loads)
        wait_all(
            run_all([pltpu.make_async_copy(buf.at[i], outs[i], sem_out.at[i]) for i in range(k)])
        )

    shape = (plan.rows, plan.features)
    return pl.pallas_call(
        body,
        out_shape=[jax.ShapeDtypeStruct(shape, BF)] * k,
        in_specs=[HBM] * len(flat),
        out_specs=[HBM] * k,
        scratch_shapes=[
            pltpu.VMEM((k,) + shape, BF),
            pltpu.SemaphoreType.DMA((len(flat),)),
            pltpu.SemaphoreType.DMA((k,)),
        ],
        cost_estimate=cost(2 * k * plan.rows * plan.features * 2),
        name="unpack",
    )(*flat)


def wanted(plan, lists, reader, owner, z):
    live, which = jnp.int32(0), jnp.int32(0)
    for e in range(plan.bh * SEL):
        entry = lists[reader * plan.bh + e // SEL, e % SEL]
        hit = (entry >= 0) & (lax.div(entry, jnp.int32(plan.bh)) == owner)
        local = lax.rem(entry, jnp.int32(plan.bh)) ^ lax.div(z, jnp.int32(plan.per))
        live = jnp.where(hit, 1, live)
        which = jnp.where(hit, local, which)
    return live, which


def select(plan, kclean, vclean, got, lists, chunk):
    n, per, slots = plan.n, plan.per, plan.ctx

    def body(*refs):
        lists_ref, k_ref, v_ref = refs[:3]
        ins, outs = refs[3 : 2 + n], refs[2 + n : 2 + n + slots]
        buf, sem_own, sem_in, sem_out = refs[2 + n + slots :]
        me, z = lax.axis_index("ctx"), lax.axis_index("head")
        own = plan.cols(z, 0, chunk)
        loads = [
            pltpu.make_async_copy(k_ref.at[:, own], buf.at[0, 0, 0], sem_own.at[0]),
            pltpu.make_async_copy(v_ref.at[:, own], buf.at[0, 1, 0], sem_own.at[1]),
        ]
        for m in range(1, n):
            loads.append(
                pltpu.make_async_copy(
                    ins[m - 1], buf.at[m // per, :, m % per], sem_in.at[m - 1]
                )
            )
        run_all(loads)
        choice = [wanted(plan, lists_ref, me ^ s, me, z)[1] for s in range(slots)]
        wait_all(loads)
        wait_all(
            run_all(
                [
                    pltpu.make_async_copy(buf.at[choice[s]], outs[s], sem_out.at[s])
                    for s in range(slots)
                ]
            )
        )

    return pl.pallas_call(
        body,
        out_shape=[jax.ShapeDtypeStruct(plan.tile, BF)] * slots,
        in_specs=[SMEM] + [HBM] * (n + 1),
        out_specs=[HBM] * slots,
        scratch_shapes=[
            pltpu.VMEM((plan.bh,) + plan.tile, BF),
            pltpu.SemaphoreType.DMA((2,)),
            pltpu.SemaphoreType.DMA((n - 1,)),
            pltpu.SemaphoreType.DMA((slots,)),
        ],
        cost_estimate=cost((slots + plan.bh) * plan.tile_bytes),
        name="select",
    )(lists, kclean, vclean, *got)


def dot(a, b, ca, cb):
    return lax.dot_general(a, b, (((ca,), (cb,)), ((), ())), preferred_element_type=F32)


def attend(plan, noisy, got, tiles, lists, chunk):
    n, per, slots, rows, bh = plan.n, plan.per, plan.ctx, plan.rows, plan.bh
    heads = plan.width // HD
    scale = 1.0 / math.sqrt(HD)
    log2e = 1.0 / math.log(2.0)
    side = (4, rows, plan.width)

    def body(*refs):
        at = 0

        def take(count):
            nonlocal at
            at += count
            return refs[at - count : at]

        (lists_ref,) = take(1)
        own_refs = take(4)
        got_refs = take(n - 1)
        tile_refs = take(slots)
        side_refs = take(n)
        term_refs = take(slots)
        rows_in, tiles_in, rows_out, terms_out, sem_own, sem_got, sem_tile, sem_side, sem_term = (
            refs[at:]
        )
        me, z = lax.axis_index("ctx"), lax.axis_index("head")
        home = lax.div(z, jnp.int32(per))
        own = plan.cols(z, 0, chunk)
        loads = [
            pltpu.make_async_copy(own_refs[i].at[:, own], rows_in.at[i, 0, 0], sem_own.at[i])
            for i in range(4)
        ]
        loads += [
            pltpu.make_async_copy(
                got_refs[m - 1], rows_in.at[:, m // per, m % per], sem_got.at[m - 1]
            )
            for m in range(1, n)
        ]
        loads += [
            pltpu.make_async_copy(tile_refs[s], tiles_in.at[s], sem_tile.at[s])
            for s in range(slots)
        ]
        run_all(loads)
        wait_all(loads)

        def step(i, carry):
            h, b = lax.div(i, jnp.int32(bh)), lax.rem(i, jnp.int32(bh))
            cols = pl.ds(pl.multiple_of(h * HD, HD), HD)

            def block(ref, *index):
                return ref[(*index, slice(None), slice(None), cols)].reshape(BLK, HD)

            def put(ref, value, *index):
                ref[(*index, slice(None), slice(None), cols)] = value.astype(BF).reshape(
                    per, rows, HD
                )

            q, k0, v0, g = (block(rows_in, j, b) for j in range(4))
            row = me * bh + (b ^ home)
            keys, values, bias, target = [k0], [v0], [None], []
            for s in range(SEL):
                entry = lists_ref[row, s]
                live = entry >= 0
                slot = jnp.where(live, lax.div(entry, jnp.int32(bh)) ^ me, 0)
                keys.append(block(tiles_in, slot, 0))
                values.append(block(tiles_in, slot, 1))
                bias.append(jnp.where(live, 0.0, MASKED).astype(F32))
                target.append(jnp.where(live, slot, slots))
            scores = []
            for kt, extra in zip(keys, bias):
                s = dot(kt, q, 1, 1) * (scale * log2e)
                scores.append(s if extra is None else s + extra)
            top = functools.reduce(
                jnp.maximum, [jnp.max(s, axis=0, keepdims=True) for s in scores]
            )
            weights = [jnp.exp2(s - top) for s in scores]
            total = functools.reduce(
                jnp.add, [jnp.sum(w, axis=0, keepdims=True) for w in weights]
            )
            inverse = 1.0 / total
            probs = [w * inverse for w in weights]
            probs_bf = [p.astype(BF) for p in probs]
            out_t = functools.reduce(
                jnp.add, [dot(vt.T, p, 1, 0) for vt, p in zip(values, probs_bf)]
            )
            out_bf = out_t.astype(BF)
            put(rows_out, out_bf.T, 0, b)
            delta = jnp.sum(g.T.astype(F32) * out_bf.astype(F32), axis=0, keepdims=True)
            dq_t = jnp.zeros((HD, BLK), F32)
            for t in range(1 + SEL):
                ds = (probs[t] * (dot(values[t], g, 1, 1) - delta)).astype(BF)
                dq_t = dq_t + dot(keys[t].T, ds, 1, 0)
                kterm = dot(ds, q, 1, 0) * scale
                vterm = dot(probs_bf[t], g, 1, 0)
                if t == 0:
                    put(rows_out, kterm, 2, b)
                    put(rows_out, vterm, 3, b)
                else:
                    put(terms_out, kterm, target[t - 1], 0)
                    put(terms_out, vterm, target[t - 1], 1)
            put(rows_out, (dq_t * scale).astype(BF).T, 1, b)
            return carry

        lax.fori_loop(0, heads * bh, step, 0)
        stores = [
            pltpu.make_async_copy(terms_out.at[s], term_refs[s], sem_term.at[s])
            for s in range(slots)
        ]
        stores += [
            pltpu.make_async_copy(rows_out.at[:, m // per, m % per], side_refs[m], sem_side.at[m])
            for m in range(n)
        ]
        run_all(stores)
        wait_all(stores)

    flops = heads * bh * 6 * 2 * BLK * (1 + SEL) * BLK * HD
    result = pl.pallas_call(
        body,
        out_shape=[jax.ShapeDtypeStruct(side, BF)] * n
        + [jax.ShapeDtypeStruct(plan.tile, BF)] * slots,
        in_specs=[SMEM] + [HBM] * (4 + n - 1 + slots),
        out_specs=[HBM] * (n + slots),
        scratch_shapes=[
            pltpu.VMEM((4, bh, per, rows, plan.width), BF),
            pltpu.VMEM((slots,) + plan.tile, BF),
            pltpu.VMEM((4, bh, per, rows, plan.width), BF),
            pltpu.VMEM((slots + 1,) + plan.tile, BF),
            pltpu.SemaphoreType.DMA((4,)),
            pltpu.SemaphoreType.DMA((n - 1,)),
            pltpu.SemaphoreType.DMA((slots,)),
            pltpu.SemaphoreType.DMA((n,)),
            pltpu.SemaphoreType.DMA((slots,)),
        ],
        compiler_params=pltpu.CompilerParams(vmem_limit_bytes=48 * 1024 * 1024),
        cost_estimate=cost(
            2 * (slots * plan.tile_bytes + 4 * bh * BLK * plan.width * 2),
            flops,
            heads * bh * BLK * (1 + SEL) * BLK,
        ),
        name="attend",
    )(lists, *noisy, *got, *tiles)
    return result[:n], result[n:]


def total_terms(plan, terms, lists):
    n, per, slots, rows, bh = plan.n, plan.per, plan.ctx, plan.rows, plan.bh

    def body(*refs):
        lists_ref, ins, outs = refs[0], refs[1 : 1 + slots], refs[1 + slots : 1 + slots + n]
        buf, summed, sem_in, sem_out = refs[1 + slots + n :]
        me, z = lax.axis_index("ctx"), lax.axis_index("head")
        loads = run_all(
            [pltpu.make_async_copy(ins[s], buf.at[s], sem_in.at[s]) for s in range(slots)]
        )
        asked = [wanted(plan, lists_ref, me ^ s, me, z) for s in range(slots)]
        wait_all(loads)
        stripe = math.gcd(rows, 32)

        def step(i, carry):
            at = pl.ds(pl.multiple_of(i * stripe, stripe), stripe)
            for kv in range(2):
                for p in range(per):
                    parts = [buf[s, kv, p, at, :].astype(F32) for s in range(slots)]
                    for j in range(bh):
                        acc = jnp.zeros((stripe, plan.width), F32)
                        for (live, which), part in zip(asked, parts):
                            acc = acc + jnp.where((live > 0) & (which == j), part, 0.0)
                        summed[j, kv, p, at, :] = acc.astype(BF)
            return carry

        lax.fori_loop(0, rows // stripe, step, 0)
        wait_all(
            run_all(
                [
                    pltpu.make_async_copy(summed.at[m // per, :, m % per], outs[m], sem_out.at[m])
                    for m in range(n)
                ]
            )
        )

    shape = (2, rows, plan.width)
    return pl.pallas_call(
        body,
        out_shape=[jax.ShapeDtypeStruct(shape, BF)] * n,
        in_specs=[SMEM] + [HBM] * slots,
        out_specs=[HBM] * n,
        scratch_shapes=[
            pltpu.VMEM((slots,) + plan.tile, BF),
            pltpu.VMEM((bh,) + plan.tile, BF),
            pltpu.SemaphoreType.DMA((slots,)),
            pltpu.SemaphoreType.DMA((n,)),
        ],
        cost_estimate=cost((slots + bh) * plan.tile_bytes),
        name="total_terms",
    )(lists, *terms)


def slot_order(slots):
    return sorted(range(1, slots), key=lambda s: (-bin(s >> 1).count("1"), s >> 1 == 0, s))


def over_head(parts):
    got = {}
    for m in range(len(parts), 0, -1):
        got[m] = swap(parts[m - 1], "head", m)
    return [got[m] for m in range(1, len(parts) + 1)]


def over_ctx(parts):
    got = {}
    for s in slot_order(len(parts)):
        got[s] = swap(parts[s], "ctx", s)
    return [parts[0]] + [got[s] for s in range(1, len(parts))]


def shards(query, key, value, kclean, vclean, grad, lists):
    plan = Plan(query.shape[0], query.shape[1], lists.shape[0], CHUNKS)
    noisy = (query, key, value, grad)
    chunks = range(plan.chunks)
    got_clean = [over_head(pack(plan, (kclean, vclean), c)) for c in chunks]
    got_noisy = [over_head(pack(plan, noisy, c)) for c in chunks]
    tiles = [over_ctx(select(plan, kclean, vclean, got_clean[c], lists, c)) for c in chunks]
    sides, cleans = [], []
    for c in chunks:
        side, terms = attend(plan, noisy, got_noisy[c], tiles[c], lists, c)
        sides.append([side[0]] + over_head(side[1:]))
        terms = over_ctx(terms)
        clean = total_terms(plan, terms, lists)
        cleans.append([clean[0]] + over_head(clean[1:]))
    return (*unpack(plan, sides, 4), *unpack(plan, cleans, 2))


def solution(mesh):
    rows = P(("ctx", "head"), None)
    return jax.shard_map(
        shards,
        mesh=mesh,
        in_specs=(rows,) * 6 + (P(),),
        out_specs=(rows,) * 6,
        check_vma=False,
    )
```

```python
import functools
import math

import jax
import jax.numpy as jnp
from jax import lax
from jax.experimental import pallas as pl
from jax.experimental.pallas import tpu as pltpu
from jax.sharding import PartitionSpec as P

HD = 128
BLK = 256
SEL = 4
CHUNKS = 2

MASKED = -1e30
BF = jnp.bfloat16
F32 = jnp.float32


HBM = pl.BlockSpec(memory_space=pl.ANY)
SMEM = pl.BlockSpec(memory_space=pltpu.SMEM)
VMEM = pl.BlockSpec(memory_space=pltpu.VMEM)


def cost(nbytes, flops=0, trans=0):
    return pl.CostEstimate(flops=flops, bytes_accessed=nbytes, transcendentals=trans)


def swap(x, axis, mask):
    count = lax.axis_size(axis)
    return lax.ppermute(x, axis, [(i, i ^ mask) for i in range(count)])


class Plan:
    def __init__(self, rows, features, blocks, chunks):
        self.ctx = lax.axis_size("ctx")
        self.n = lax.axis_size("head")
        self.rows = rows
        self.features = features
        self.bh = blocks // self.ctx
        self.per = self.n // self.bh
        self.group = features // self.n
        self.heads = self.group // HD
        self.chunks = min(chunks, self.heads)
        self.width = self.group // self.chunks
        self.tile = (2, self.per, rows, self.width)
        self.tile_bytes = 2 * BLK * self.width * 2

    def cols(self, z, mask, chunk):
        start = (z ^ mask) * self.group + chunk * self.width
        return pl.ds(pl.multiple_of(start, HD), self.width)


def run_all(copies):
    for c in copies:
        c.start()
    for c in copies:
        c.wait()


def on_chip(arrays):
    return [pltpu.with_memory_space_constraint(x, pltpu.VMEM) for x in arrays]


def grant(mib):
    return pltpu.CompilerParams(vmem_limit_bytes=mib * 1024 * 1024)


def pack(plan, arrays, chunk):
    k, n = len(arrays), plan.n

    def body(*refs):
        ins, outs, sem = refs[:k], refs[k : k + n], refs[k + n]
        z = lax.axis_index("head")
        run_all(
            [
                pltpu.make_async_copy(
                    ins[i].at[:, plan.cols(z, m, chunk)], outs[m].at[i], sem.at[m, i]
                )
                for m in range(n)
                for i in range(k)
            ]
        )

    shape = (k, plan.rows, plan.width)
    return pl.pallas_call(
        body,
        out_shape=[pltpu.VMEM(shape, BF)] * n,
        in_specs=[HBM] * k,
        out_specs=[VMEM] * n,
        scratch_shapes=[pltpu.SemaphoreType.DMA((n, k))],
        compiler_params=grant(1),
        cost_estimate=cost(2 * k * n * plan.rows * plan.width * 2),
        name="pack",
    )(*arrays)


def unpack(plan, pieces, k):
    n, chunks = plan.n, plan.chunks
    flat = [p for chunk in pieces for p in chunk]

    def body(*refs):
        ins, outs, sem = refs[: n * chunks], refs[n * chunks : n * chunks + k], refs[-1]
        z = lax.axis_index("head")
        run_all(
            [
                pltpu.make_async_copy(
                    ins[c * n + m].at[i], outs[i].at[:, plan.cols(z, m, c)], sem.at[c * n + m, i]
                )
                for c in range(chunks)
                for m in range(n)
                for i in range(k)
            ]
        )

    shape = (plan.rows, plan.features)
    return pl.pallas_call(
        body,
        out_shape=[jax.ShapeDtypeStruct(shape, BF)] * k,
        in_specs=[VMEM] * len(flat),
        out_specs=[HBM] * k,
        scratch_shapes=[pltpu.SemaphoreType.DMA((len(flat), k))],
        compiler_params=grant(1),
        cost_estimate=cost(2 * k * plan.rows * plan.features * 2),
        name="unpack",
    )(*on_chip(flat))


def wanted(plan, lists, reader, owner, z):
    live, which = jnp.int32(0), jnp.int32(0)
    for e in range(plan.bh * SEL):
        entry = lists[reader * plan.bh + e // SEL, e % SEL]
        hit = (entry >= 0) & (lax.div(entry, jnp.int32(plan.bh)) == owner)
        local = lax.rem(entry, jnp.int32(plan.bh)) ^ lax.div(z, jnp.int32(plan.per))
        live = jnp.where(hit, 1, live)
        which = jnp.where(hit, local, which)
    return live, which


def select(plan, rows, lists):
    n, per, slots, bh = plan.n, plan.per, plan.ctx, plan.bh

    def body(*refs):
        lists_ref, ins, outs = refs[0], refs[1 : 1 + n], refs[1 + n :]
        me, z = lax.axis_index("ctx"), lax.axis_index("head")
        for s in range(slots):
            which = wanted(plan, lists_ref, me ^ s, me, z)[1]
            for j in range(bh):

                @pl.when(which == j)
                def _():
                    for p in range(per):
                        outs[s][:, p] = ins[j * per + p][...]

    return pl.pallas_call(
        body,
        out_shape=[pltpu.VMEM(plan.tile, BF)] * slots,
        in_specs=[SMEM] + [VMEM] * n,
        out_specs=[VMEM] * slots,
        compiler_params=grant(1),
        cost_estimate=cost((slots + plan.bh) * plan.tile_bytes),
        name="select",
    )(lists, *on_chip(rows))


def dot(a, b, ca, cb):
    return lax.dot_general(a, b, (((ca,), (cb,)), ((), ())), preferred_element_type=F32)


def attend(plan, noisy, tiles, lists):
    n, per, slots, rows, bh = plan.n, plan.per, plan.ctx, plan.rows, plan.bh
    heads = plan.width // HD
    scale = 1.0 / math.sqrt(HD)
    log2e = 1.0 / math.log(2.0)
    side = (4, rows, plan.width)

    def body(*refs):
        lists_ref, rows_in, tile_refs = refs[0], refs[1 : 1 + n], refs[1 + n : 1 + n + slots]
        rows_out = refs[1 + n + slots : 1 + 2 * n + slots]
        term_refs = refs[1 + 2 * n + slots : 1 + 2 * n + 2 * slots]
        tiles_in, terms_out = refs[1 + 2 * n + 2 * slots :]
        me, z = lax.axis_index("ctx"), lax.axis_index("head")
        home = lax.div(z, jnp.int32(per))
        for s in range(slots):
            tiles_in[s] = tile_refs[s][...]

        def step(h, carry):
            cols = pl.ds(pl.multiple_of(h * HD, HD), HD)
            for b in range(bh):
                part = range(b * per, (b + 1) * per)

                def noisy_block(j):
                    return jnp.concatenate([rows_in[m][j, :, cols] for m in part], 0)

                def put_noisy(j, value):
                    value = value.astype(BF).reshape(per, rows, HD)
                    for p in range(per):
                        rows_out[b * per + p][j, :, cols] = value[p]

                def clean_block(slot, kv):
                    return tiles_in[slot, kv, :, :, cols].reshape(BLK, HD)

                def put_clean(slot, kv, value):
                    terms_out[slot, kv, :, :, cols] = value.astype(BF).reshape(per, rows, HD)

                q, k0, v0, g = (noisy_block(j) for j in range(4))
                row = me * bh + (b ^ home)
                keys, values, bias, target = [k0], [v0], [None], []
                for s in range(SEL):
                    entry = lists_ref[row, s]
                    live = entry >= 0
                    slot = jnp.where(live, lax.div(entry, jnp.int32(bh)) ^ me, 0)
                    keys.append(clean_block(slot, 0))
                    values.append(clean_block(slot, 1))
                    bias.append(jnp.where(live, 0.0, MASKED).astype(F32))
                    target.append(jnp.where(live, slot, slots))
                scores = []
                for kt, extra in zip(keys, bias):
                    s = dot(kt, q, 1, 1) * (scale * log2e)
                    scores.append(s if extra is None else s + extra)
                top = functools.reduce(
                    jnp.maximum, [jnp.max(s, axis=0, keepdims=True) for s in scores]
                )
                weights = [jnp.exp2(s - top) for s in scores]
                total = functools.reduce(
                    jnp.add, [jnp.sum(w, axis=0, keepdims=True) for w in weights]
                )
                inverse = 1.0 / total
                probs = [w * inverse for w in weights]
                probs_bf = [p.astype(BF) for p in probs]
                out_t = functools.reduce(
                    jnp.add, [dot(vt.T, p, 1, 0) for vt, p in zip(values, probs_bf)]
                )
                out_bf = out_t.astype(BF)
                put_noisy(0, out_bf.T)
                delta = jnp.sum(g.T.astype(F32) * out_bf.astype(F32), axis=0, keepdims=True)
                dq_t = jnp.zeros((HD, BLK), F32)
                for t in range(1 + SEL):
                    ds = (probs[t] * (dot(values[t], g, 1, 1) - delta)).astype(BF)
                    dq_t = dq_t + dot(keys[t].T, ds, 1, 0)
                    kterm = dot(ds, q, 1, 0) * scale
                    vterm = dot(probs_bf[t], g, 1, 0)
                    if t == 0:
                        put_noisy(2, kterm)
                        put_noisy(3, vterm)
                    else:
                        put_clean(target[t - 1], 0, kterm)
                        put_clean(target[t - 1], 1, vterm)
                put_noisy(1, (dq_t * scale).astype(BF).T)
            return carry

        lax.fori_loop(0, heads, step, 0)
        for s in range(slots):
            term_refs[s][...] = terms_out[s]

    flops = heads * bh * 6 * 2 * BLK * (1 + SEL) * BLK * HD
    result = pl.pallas_call(
        body,
        out_shape=[pltpu.VMEM(side, BF)] * n + [pltpu.VMEM(plan.tile, BF)] * slots,
        in_specs=[SMEM] + [VMEM] * (n + slots),
        out_specs=[VMEM] * (n + slots),
        scratch_shapes=[
            pltpu.VMEM((slots,) + plan.tile, BF),
            pltpu.VMEM((slots + 1,) + plan.tile, BF),
        ],
        compiler_params=grant(24),
        cost_estimate=cost(
            2 * (slots * plan.tile_bytes + 4 * bh * BLK * plan.width * 2),
            flops,
            heads * bh * BLK * (1 + SEL) * BLK,
        ),
        name="attend",
    )(lists, *on_chip(noisy), *on_chip(tiles))
    return result[:n], result[n:]


def total_terms(plan, terms, lists):
    n, per, slots, rows, bh = plan.n, plan.per, plan.ctx, plan.rows, plan.bh

    def body(*refs):
        lists_ref, ins, outs = refs[0], refs[1 : 1 + slots], refs[1 + slots :]
        me, z = lax.axis_index("ctx"), lax.axis_index("head")
        asked = [wanted(plan, lists_ref, me ^ s, me, z) for s in range(slots)]
        stripe = math.gcd(rows, 32)

        def step(i, carry):
            at = pl.ds(pl.multiple_of(i * stripe, stripe), stripe)
            for kv in range(2):
                for p in range(per):
                    parts = [ins[s][kv, p, at, :].astype(F32) for s in range(slots)]
                    for j in range(bh):
                        acc = jnp.zeros((stripe, plan.width), F32)
                        for (live, which), part in zip(asked, parts):
                            acc = acc + jnp.where((live > 0) & (which == j), part, 0.0)
                        outs[j * per + p][kv, at, :] = acc.astype(BF)
            return carry

        lax.fori_loop(0, rows // stripe, step, 0)

    shape = (2, rows, plan.width)
    return pl.pallas_call(
        body,
        out_shape=[pltpu.VMEM(shape, BF)] * n,
        in_specs=[SMEM] + [VMEM] * slots,
        out_specs=[VMEM] * n,
        compiler_params=grant(4),
        cost_estimate=cost((slots + bh) * plan.tile_bytes),
        name="total_terms",
    )(lists, *on_chip(terms))


def slot_order(slots):
    return sorted(range(1, slots), key=lambda s: (-bin(s >> 1).count("1"), s >> 1 == 0, s))


def over_head(parts):
    got = {0: parts[0]}
    for m in range(len(parts) - 1, 0, -1):
        got[m] = swap(parts[m], "head", m)
    return [got[m] for m in range(len(parts))]


def over_ctx(parts):
    got = {0: parts[0]}
    for s in slot_order(len(parts)):
        got[s] = swap(parts[s], "ctx", s)
    return [got[s] for s in range(len(parts))]


def shards(query, key, value, kclean, vclean, grad, lists):
    plan = Plan(query.shape[0], query.shape[1], lists.shape[0], CHUNKS)
    chunks = range(plan.chunks)
    clean = [over_head(pack(plan, (kclean, vclean), c)) for c in chunks]
    noisy = [over_head(pack(plan, (query, key, value, grad), c)) for c in chunks]
    tiles = [over_ctx(select(plan, clean[c], lists)) for c in chunks]
    sides, sums = [], []
    for c in chunks:
        side, terms = attend(plan, noisy[c], tiles[c], lists)
        sides.append(over_head(side))
        terms = over_ctx(terms)
        sums.append(over_head(total_terms(plan, terms, lists)))
    return (*unpack(plan, sides, 4), *unpack(plan, sums, 2))


def solution(mesh):
    rows = P(("ctx", "head"), None)
    return jax.shard_map(
        shards,
        mesh=mesh,
        in_specs=(rows,) * 6 + (P(),),
        out_specs=(rows,) * 6,
        check_vma=False,
    )
```

```python
import functools
import math

import jax
import jax.numpy as jnp
from jax import lax
from jax.experimental import pallas as pl
from jax.experimental.pallas import tpu as pltpu
from jax.sharding import PartitionSpec as P

HD = 128
BLK = 256
SEL = 4
STATS = 16
CHUNKS = 2

MASKED = -1e30
BF = jnp.bfloat16
F32 = jnp.float32


HBM = pl.BlockSpec(memory_space=pl.ANY)
SMEM = pl.BlockSpec(memory_space=pltpu.SMEM)
VMEM = pl.BlockSpec(memory_space=pltpu.VMEM)


def cost(nbytes, flops=0, trans=0):
    return pl.CostEstimate(flops=flops, bytes_accessed=nbytes, transcendentals=trans)


def swap(x, axis, mask):
    count = lax.axis_size(axis)
    return lax.ppermute(x, axis, [(i, i ^ mask) for i in range(count)])


class Plan:
    def __init__(self, rows, features, blocks, chunks):
        self.ctx = lax.axis_size("ctx")
        self.n = lax.axis_size("head")
        self.rows = rows
        self.features = features
        self.bh = blocks // self.ctx
        self.per = self.n // self.bh
        self.group = features // self.n
        self.heads = self.group // HD
        self.chunks = min(chunks, self.heads)
        self.width = self.group // self.chunks
        self.tile = (2, self.per, rows, self.width)
        self.tile_bytes = 2 * BLK * self.width * 2

    def cols(self, z, mask, chunk):
        start = (z ^ mask) * self.group + chunk * self.width
        return pl.ds(pl.multiple_of(start, HD), self.width)


def run_all(copies):
    for c in copies:
        c.start()
    for c in copies:
        c.wait()


def on_chip(arrays):
    return [pltpu.with_memory_space_constraint(x, pltpu.VMEM) for x in arrays]


def grant(mib):
    return pltpu.CompilerParams(vmem_limit_bytes=mib * 1024 * 1024)


def pack(plan, arrays, chunk):
    k, n = len(arrays), plan.n

    def body(*refs):
        ins, outs, sem = refs[:k], refs[k : k + n], refs[k + n]
        z = lax.axis_index("head")
        run_all(
            [
                pltpu.make_async_copy(
                    ins[i].at[:, plan.cols(z, m, chunk)], outs[m].at[i], sem.at[m, i]
                )
                for m in range(n)
                for i in range(k)
            ]
        )

    shape = (k, plan.rows, plan.width)
    return pl.pallas_call(
        body,
        out_shape=[pltpu.VMEM(shape, BF)] * n,
        in_specs=[HBM] * k,
        out_specs=[VMEM] * n,
        scratch_shapes=[pltpu.SemaphoreType.DMA((n, k))],
        compiler_params=grant(1),
        cost_estimate=cost(2 * k * n * plan.rows * plan.width * 2),
        name="pack",
    )(*(pltpu.with_memory_space_constraint(x, pltpu.HBM) for x in arrays))


def unpack(plan, pieces, k):
    n, chunks = plan.n, plan.chunks
    flat = [p for chunk in pieces for p in chunk]

    def body(*refs):
        ins, outs, sem = refs[: n * chunks], refs[n * chunks : n * chunks + k], refs[-1]
        z = lax.axis_index("head")
        run_all(
            [
                pltpu.make_async_copy(
                    ins[c * n + m].at[i], outs[i].at[:, plan.cols(z, m, c)], sem.at[c * n + m, i]
                )
                for c in range(chunks)
                for m in range(n)
                for i in range(k)
            ]
        )

    shape = (plan.rows, plan.features)
    return pl.pallas_call(
        body,
        out_shape=[jax.ShapeDtypeStruct(shape, BF)] * k,
        in_specs=[VMEM] * len(flat),
        out_specs=[HBM] * k,
        scratch_shapes=[pltpu.SemaphoreType.DMA((len(flat), k))],
        compiler_params=grant(1),
        cost_estimate=cost(2 * k * plan.rows * plan.features * 2),
        name="unpack",
    )(*on_chip(flat))


def wanted(plan, lists, reader, owner, z):
    live, which = jnp.int32(0), jnp.int32(0)
    for e in range(plan.bh * SEL):
        entry = lists[reader * plan.bh + e // SEL, e % SEL]
        hit = (entry >= 0) & (lax.div(entry, jnp.int32(plan.bh)) == owner)
        local = lax.rem(entry, jnp.int32(plan.bh)) ^ lax.div(z, jnp.int32(plan.per))
        live = jnp.where(hit, 1, live)
        which = jnp.where(hit, local, which)
    return live, which


def select(plan, rows, lists):
    n, per, slots, bh = plan.n, plan.per, plan.ctx, plan.bh

    def body(*refs):
        lists_ref, ins, outs = refs[0], refs[1 : 1 + n], refs[1 + n :]
        me, z = lax.axis_index("ctx"), lax.axis_index("head")
        for s in range(slots):
            which = wanted(plan, lists_ref, me ^ s, me, z)[1]
            for j in range(bh):

                @pl.when(which == j)
                def _():
                    for p in range(per):
                        outs[s][:, p] = ins[j * per + p][...]

    return pl.pallas_call(
        body,
        out_shape=[pltpu.VMEM(plan.tile, BF)] * slots,
        in_specs=[SMEM] + [VMEM] * n,
        out_specs=[VMEM] * slots,
        compiler_params=grant(1),
        cost_estimate=cost((slots + plan.bh) * plan.tile_bytes),
        name="select",
    )(lists, *on_chip(rows))


def dot(a, b, ca, cb):
    return lax.dot_general(a, b, (((ca,), (cb,)), ((), ())), preferred_element_type=F32)


def stat_rows(*vectors):
    pieces = []
    for v in vectors:
        for _ in range(3):
            piece = v.astype(BF)
            v = v - piece.astype(F32)
            pieces += [piece.astype(F32)[:, i : i + HD] for i in range(0, BLK, HD)]
    pieces.append(jnp.zeros((STATS - len(pieces), HD), F32))
    return jnp.concatenate(pieces, 0).astype(BF)


def read_stats(rows, count):
    rows, wide, vectors = rows.astype(F32), BLK // HD, []
    for v in range(count):
        at = v * 3 * wide
        parts = [
            rows[at + i : at + i + 1]
            + rows[at + wide + i : at + wide + i + 1]
            + rows[at + 2 * wide + i : at + 2 * wide + i + 1]
            for i in range(wide)
        ]
        vectors.append(jnp.concatenate(parts, 1))
    return vectors


def attend(plan, noisy, tiles, lists):
    n, per, slots, rows, bh = plan.n, plan.per, plan.ctx, plan.rows, plan.bh
    heads = plan.width // HD
    scale = 1.0 / math.sqrt(HD)
    log2e = 1.0 / math.log(2.0)
    side = (2 * rows + STATS, plan.width)

    def body(*refs):
        lists_ref, rows_in, tile_refs = refs[0], refs[1 : 1 + n], refs[1 + n : 1 + n + slots]
        rows_out = refs[1 + n + slots : 1 + 2 * n + slots]
        term_refs = refs[1 + 2 * n + slots : 1 + 2 * n + 2 * slots]
        tiles_in, terms_out = refs[1 + 2 * n + 2 * slots :]
        me, z = lax.axis_index("ctx"), lax.axis_index("head")
        home = lax.div(z, jnp.int32(per))
        for s in range(slots):
            tiles_in[s] = tile_refs[s][...]

        def step(h, carry):
            cols = pl.ds(pl.multiple_of(h * HD, HD), HD)
            for b in range(bh):
                part = range(b * per, (b + 1) * per)

                def noisy_block(j):
                    return jnp.concatenate([rows_in[m][j, :, cols] for m in part], 0)

                def put_noisy(j, value):
                    value = value.astype(BF).reshape(per, rows, HD)
                    for p in range(per):
                        rows_out[b * per + p][j * rows : (j + 1) * rows, cols] = value[p]

                def clean_block(slot, kv):
                    return tiles_in[slot, kv, :, :, cols].reshape(BLK, HD)

                def put_clean(slot, kv, value):
                    terms_out[slot, kv, :, :, cols] = value.astype(BF).reshape(per, rows, HD)

                q, k0, v0, g = (noisy_block(j) for j in range(4))
                row = me * bh + (b ^ home)
                keys, values, bias, target = [k0], [v0], [None], []
                for s in range(SEL):
                    entry = lists_ref[row, s]
                    live = entry >= 0
                    slot = jnp.where(live, lax.div(entry, jnp.int32(bh)) ^ me, 0)
                    keys.append(clean_block(slot, 0))
                    values.append(clean_block(slot, 1))
                    bias.append(jnp.where(live, 0.0, MASKED).astype(F32))
                    target.append(jnp.where(live, slot, slots))
                scores = []
                for kt, extra in zip(keys, bias):
                    s = dot(kt, q, 1, 1) * (scale * log2e)
                    scores.append(s if extra is None else s + extra)
                top = functools.reduce(
                    jnp.maximum, [jnp.max(s, axis=0, keepdims=True) for s in scores]
                )
                weights = [jnp.exp2(s - top) for s in scores]
                total = functools.reduce(
                    jnp.add, [jnp.sum(w, axis=0, keepdims=True) for w in weights]
                )
                inverse = 1.0 / total
                log_total = top + jnp.log(total) * log2e
                probs = [w * inverse for w in weights]
                probs_bf = [p.astype(BF) for p in probs]
                out_t = functools.reduce(
                    jnp.add, [dot(vt.T, p, 1, 0) for vt, p in zip(values, probs_bf)]
                )
                out_bf = out_t.astype(BF)
                put_noisy(0, out_bf.T)
                delta = jnp.sum(g.T.astype(F32) * out_bf.astype(F32), axis=0, keepdims=True)
                stats = stat_rows(log_total, delta)
                for p in range(per):
                    rows_out[b * per + p][2 * rows :, cols] = stats
                dq_t = jnp.zeros((HD, BLK), F32)
                for t in range(1 + SEL):
                    ds = (probs[t] * (dot(values[t], g, 1, 1) - delta)).astype(BF)
                    dq_t = dq_t + dot(keys[t].T, ds, 1, 0)
                    if t > 0:
                        put_clean(target[t - 1], 0, dot(ds, q, 1, 0) * scale)
                        put_clean(target[t - 1], 1, dot(probs_bf[t], g, 1, 0))
                put_noisy(1, (dq_t * scale).astype(BF).T)
            return carry

        lax.fori_loop(0, heads, step, 0)
        for s in range(slots):
            term_refs[s][...] = terms_out[s]

    flops = heads * bh * 6 * 2 * BLK * (1 + SEL) * BLK * HD
    result = pl.pallas_call(
        body,
        out_shape=[pltpu.VMEM(side, BF)] * n + [pltpu.VMEM(plan.tile, BF)] * slots,
        in_specs=[SMEM] + [VMEM] * (n + slots),
        out_specs=[VMEM] * (n + slots),
        scratch_shapes=[
            pltpu.VMEM((slots,) + plan.tile, BF),
            pltpu.VMEM((slots + 1,) + plan.tile, BF),
        ],
        compiler_params=grant(24),
        cost_estimate=cost(
            2 * (slots * plan.tile_bytes + 4 * bh * BLK * plan.width * 2),
            flops,
            heads * bh * BLK * (1 + SEL) * BLK,
        ),
        name="attend",
    )(lists, *on_chip(noisy), *on_chip(tiles))
    return result[:n], result[n:]


def total_terms(plan, terms, lists):
    n, per, slots, rows, bh = plan.n, plan.per, plan.ctx, plan.rows, plan.bh

    def body(*refs):
        lists_ref, ins, outs = refs[0], refs[1 : 1 + slots], refs[1 + slots :]
        me, z = lax.axis_index("ctx"), lax.axis_index("head")
        asked = [wanted(plan, lists_ref, me ^ s, me, z) for s in range(slots)]
        stripe = math.gcd(rows, 32)

        def step(i, carry):
            at = pl.ds(pl.multiple_of(i * stripe, stripe), stripe)
            for kv in range(2):
                for p in range(per):
                    parts = [ins[s][kv, p, at, :].astype(F32) for s in range(slots)]
                    for j in range(bh):
                        acc = jnp.zeros((stripe, plan.width), F32)
                        for (live, which), part in zip(asked, parts):
                            acc = acc + jnp.where((live > 0) & (which == j), part, 0.0)
                        outs[j * per + p][kv, at, :] = acc.astype(BF)
            return carry

        lax.fori_loop(0, rows // stripe, step, 0)

    shape = (2, rows, plan.width)
    return pl.pallas_call(
        body,
        out_shape=[pltpu.VMEM(shape, BF)] * n,
        in_specs=[SMEM] + [VMEM] * slots,
        out_specs=[VMEM] * n,
        compiler_params=grant(4),
        cost_estimate=cost((slots + bh) * plan.tile_bytes),
        name="total_terms",
    )(lists, *on_chip(terms))


def finish(plan, sides, query, grad, key, value):
    n, per, rows, chunks = plan.n, plan.per, plan.rows, plan.chunks
    flat = [p for chunk in sides for p in chunk]
    heads = plan.width // HD
    scale = 1.0 / math.sqrt(HD)
    log2e = 1.0 / math.log(2.0)

    def body(*refs):
        ins, at = refs[: n * chunks], n * chunks
        q_refs, g_refs = refs[at : at + per], refs[at + per : at + 2 * per]
        k_ref, v_ref = refs[at + 2 * per : at + 2 * per + 2]
        outs = refs[at + 2 * per + 2 : at + 2 * per + 6]
        dk_buf, dv_buf, sem, sem_own = refs[at + 2 * per + 6 :]
        z = lax.axis_index("head")
        moves = [
            pltpu.make_async_copy(
                ins[c * n + m].at[pl.ds(j * rows, rows), :],
                outs[j].at[:, plan.cols(z, m, c)],
                sem.at[c * n + m, j],
            )
            for c in range(chunks)
            for m in range(n)
            for j in range(2)
        ]
        for move in moves:
            move.start()
        for c in range(chunks):
            for m in range(n):
                order = [p ^ (m % per) for p in range(per)]
                start = (z ^ m) * plan.group + c * plan.width
                for h in range(heads):
                    cols = pl.ds(pl.multiple_of(start + h * HD, HD), HD)
                    q = jnp.concatenate([q_refs[p][:, cols] for p in order], 0)
                    g = jnp.concatenate([g_refs[p][:, cols] for p in order], 0)
                    log_total, delta = read_stats(
                        ins[c * n + m][2 * rows :, h * HD : (h + 1) * HD], 2
                    )
                    s = dot(k_ref[:, cols], q, 1, 1) * (scale * log2e)
                    prob = jnp.exp2(s - log_total)
                    ds = prob * (dot(v_ref[:, cols], g, 1, 1) - delta)
                    dk_buf[:, cols] = (dot(ds.astype(BF), q, 1, 0) * scale).astype(BF)
                    dv_buf[:, cols] = dot(prob.astype(BF), g, 1, 0).astype(BF)
        own = [
            pltpu.make_async_copy(dk_buf, outs[2], sem_own.at[0]),
            pltpu.make_async_copy(dv_buf, outs[3], sem_own.at[1]),
        ]
        run_all(own)
        for move in moves:
            move.wait()

    shape = (rows, plan.features)
    return pl.pallas_call(
        body,
        out_shape=[jax.ShapeDtypeStruct(shape, BF)] * 4,
        in_specs=[VMEM] * (len(flat) + 2 * per + 2),
        out_specs=[HBM] * 4,
        scratch_shapes=[
            pltpu.VMEM(shape, BF),
            pltpu.VMEM(shape, BF),
            pltpu.SemaphoreType.DMA((len(flat), 2)),
            pltpu.SemaphoreType.DMA((2,)),
        ],
        compiler_params=grant(6),
        cost_estimate=cost(
            12 * rows * plan.features * 2, 4 * 2 * rows * BLK * plan.features, rows * BLK * 16
        ),
        name="finish",
    )(*on_chip(flat), *on_chip(query), *on_chip(grad), *on_chip([key, value]))


def slot_order(slots):
    return sorted(range(1, slots), key=lambda s: (-bin(s >> 1).count("1"), s >> 1 == 0, s))


def over_head(parts):
    got = {0: parts[0]}
    for m in range(len(parts) - 1, 0, -1):
        got[m] = swap(parts[m], "head", m)
    return [got[m] for m in range(len(parts))]


def over_ctx(parts):
    got = {0: parts[0]}
    for s in slot_order(len(parts)):
        got[s] = swap(parts[s], "ctx", s)
    return [got[s] for s in range(len(parts))]


def shards(query, key, value, kclean, vclean, grad, lists):
    plan = Plan(query.shape[0], query.shape[1], lists.shape[0], CHUNKS)
    chunks = range(plan.chunks)
    clean = [over_head(pack(plan, (kclean, vclean), c)) for c in chunks]
    noisy = [over_head(pack(plan, (query, key, value, grad), c)) for c in chunks]
    tiles = [over_ctx(select(plan, clean[c], lists)) for c in chunks]
    sides, sums = [], []
    for c in chunks:
        side, terms = attend(plan, noisy[c], tiles[c], lists)
        sides.append(over_head(side))
        terms = over_ctx(terms)
        sums.append(over_head(total_terms(plan, terms, lists)))
    masks = range(plan.per)
    block_q = [query if m == 0 else swap(query, "head", m) for m in masks]
    block_g = [grad if m == 0 else swap(grad, "head", m) for m in masks]
    rows = finish(plan, sides, block_q, block_g, key, value)
    return (*rows, *unpack(plan, sums, 2))


def solution(mesh):
    rows = P(("ctx", "head"), None)
    return jax.shard_map(
        shards,
        mesh=mesh,
        in_specs=(rows,) * 6 + (P(),),
        out_specs=(rows,) * 6,
        check_vma=False,
    )
```

```python
import functools
import math

import jax
import jax.numpy as jnp
from jax import lax
from jax.experimental import pallas as pl
from jax.experimental.pallas import tpu as pltpu
from jax.sharding import PartitionSpec as P

HD = 128
BLK = 256
SEL = 4
STATS = 16
CHUNKS = 2
RELAYED = (0,)

MASKED = -1e30
BF = jnp.bfloat16
F32 = jnp.float32


HBM = pl.BlockSpec(memory_space=pl.ANY)
SMEM = pl.BlockSpec(memory_space=pltpu.SMEM)
VMEM = pl.BlockSpec(memory_space=pltpu.VMEM)


def cost(nbytes, flops=0, trans=0):
    return pl.CostEstimate(flops=flops, bytes_accessed=nbytes, transcendentals=trans)


def swap(x, axis, mask):
    count = lax.axis_size(axis)
    return lax.ppermute(x, axis, [(i, i ^ mask) for i in range(count)])


class Plan:
    def __init__(self, rows, features, blocks, chunks):
        self.ctx = lax.axis_size("ctx")
        self.n = lax.axis_size("head")
        self.rows = rows
        self.features = features
        self.bh = blocks // self.ctx
        self.per = self.n // self.bh
        self.group = features // self.n
        self.heads = self.group // HD
        self.chunks = min(chunks, self.heads)
        self.width = self.group // self.chunks
        self.tile = (2, self.per, rows, self.width)
        self.tile_bytes = 2 * BLK * self.width * 2

    def cols(self, z, mask, chunk):
        start = (z ^ mask) * self.group + chunk * self.width
        return pl.ds(pl.multiple_of(start, HD), self.width)


def run_all(copies):
    for c in copies:
        c.start()
    for c in copies:
        c.wait()


def on_chip(arrays):
    return [pltpu.with_memory_space_constraint(x, pltpu.VMEM) for x in arrays]


def grant(mib):
    return pltpu.CompilerParams(vmem_limit_bytes=mib * 1024 * 1024)


def pack(plan, arrays, chunk):
    k, n = len(arrays), plan.n

    def body(*refs):
        ins, outs, sem = refs[:k], refs[k : k + n], refs[k + n]
        z = lax.axis_index("head")
        run_all(
            [
                pltpu.make_async_copy(
                    ins[i].at[:, plan.cols(z, m, chunk)], outs[m].at[i], sem.at[m, i]
                )
                for m in range(n)
                for i in range(k)
            ]
        )

    shape = (k, plan.rows, plan.width)
    return pl.pallas_call(
        body,
        out_shape=[pltpu.VMEM(shape, BF)] * n,
        in_specs=[HBM] * k,
        out_specs=[VMEM] * n,
        scratch_shapes=[pltpu.SemaphoreType.DMA((n, k))],
        compiler_params=grant(1),
        cost_estimate=cost(2 * k * n * plan.rows * plan.width * 2),
        name="pack",
    )(*(pltpu.with_memory_space_constraint(x, pltpu.HBM) for x in arrays))


def unpack(plan, pieces, k):
    n, chunks = plan.n, plan.chunks
    flat = [p for chunk in pieces for p in chunk]

    def body(*refs):
        ins, outs, sem = refs[: n * chunks], refs[n * chunks : n * chunks + k], refs[-1]
        z = lax.axis_index("head")
        run_all(
            [
                pltpu.make_async_copy(
                    ins[c * n + m].at[i], outs[i].at[:, plan.cols(z, m, c)], sem.at[c * n + m, i]
                )
                for c in range(chunks)
                for m in range(n)
                for i in range(k)
            ]
        )

    shape = (plan.rows, plan.features)
    return pl.pallas_call(
        body,
        out_shape=[jax.ShapeDtypeStruct(shape, BF)] * k,
        in_specs=[VMEM] * len(flat),
        out_specs=[HBM] * k,
        scratch_shapes=[pltpu.SemaphoreType.DMA((len(flat), k))],
        compiler_params=grant(1),
        cost_estimate=cost(2 * k * plan.rows * plan.features * 2),
        name="unpack",
    )(*on_chip(flat))


def wanted(plan, lists, reader, owner, z):
    live, which = jnp.int32(0), jnp.int32(0)
    for e in range(plan.bh * SEL):
        entry = lists[reader * plan.bh + e // SEL, e % SEL]
        hit = (entry >= 0) & (lax.div(entry, jnp.int32(plan.bh)) == owner)
        local = lax.rem(entry, jnp.int32(plan.bh)) ^ lax.div(z, jnp.int32(plan.per))
        live = jnp.where(hit, 1, live)
        which = jnp.where(hit, local, which)
    return live, which


def select(plan, rows, lists):
    n, per, slots, bh = plan.n, plan.per, plan.ctx, plan.bh

    def body(*refs):
        lists_ref, ins, outs = refs[0], refs[1 : 1 + n], refs[1 + n :]
        me, z = lax.axis_index("ctx"), lax.axis_index("head")
        for s in range(slots):
            which = wanted(plan, lists_ref, me ^ s, me, z)[1]
            for j in range(bh):

                @pl.when(which == j)
                def _():
                    for p in range(per):
                        outs[s][:, p] = ins[j * per + p][...]

    return pl.pallas_call(
        body,
        out_shape=[pltpu.VMEM(plan.tile, BF)] * slots,
        in_specs=[SMEM] + [VMEM] * n,
        out_specs=[VMEM] * slots,
        compiler_params=grant(1),
        cost_estimate=cost((slots + plan.bh) * plan.tile_bytes),
        name="select",
    )(lists, *on_chip(rows))


def gather(plan, rows):
    n, per, bh = plan.n, plan.per, plan.bh

    def body(*refs):
        ins, outs = refs[:n], refs[n:]
        for j in range(bh):
            for p in range(per):
                outs[j][:, p] = ins[j * per + p][...]

    return pl.pallas_call(
        body,
        out_shape=[pltpu.VMEM(plan.tile, BF)] * bh,
        in_specs=[VMEM] * n,
        out_specs=[VMEM] * bh,
        compiler_params=grant(1),
        cost_estimate=cost(2 * bh * plan.tile_bytes),
        name="gather",
    )(*on_chip(rows))


def pick(plan, blocks, lists):
    bh, half = plan.bh, plan.ctx // 2

    def body(*refs):
        lists_ref, ins, out, note = refs[0], refs[1 : 1 + bh * half], *refs[1 + bh * half :]
        me, z = lax.axis_index("ctx"), lax.axis_index("head")
        note[...] = jnp.zeros(note.shape, F32)
        for i in range(half):
            which = wanted(plan, lists_ref, me ^ 1, me ^ (2 * i), z)[1]
            for j in range(bh):

                @pl.when(which == j)
                def _():
                    out[i] = ins[i * bh + j][...]

    return pl.pallas_call(
        body,
        out_shape=[pltpu.VMEM((half,) + plan.tile, BF), pltpu.VMEM((8, HD), F32)],
        in_specs=[SMEM] + [VMEM] * (bh * half),
        out_specs=[VMEM] * 2,
        compiler_params=grant(1),
        cost_estimate=cost(2 * half * plan.tile_bytes),
        name="pick",
    )(lists, *on_chip(blocks))[0]


def relay(plan, rows, lists):
    own = gather(plan, rows)
    near = [[swap(block, "ctx", mask) for block in own] for mask in (2, 4)]
    far = [swap(near[0][0], "ctx", 4), swap(near[1][1], "ctx", 2)]
    blocks = [*own, *near[0], *near[1], *far]
    theirs = pick(plan, blocks, lists)
    return [*blocks, swap(theirs, "ctx", 1)]


def dot(a, b, ca, cb):
    return lax.dot_general(a, b, (((ca,), (cb,)), ((), ())), preferred_element_type=F32)


def stat_rows(*vectors):
    pieces = []
    for v in vectors:
        for _ in range(3):
            piece = v.astype(BF)
            v = v - piece.astype(F32)
            pieces += [piece.astype(F32)[:, i : i + HD] for i in range(0, BLK, HD)]
    pieces.append(jnp.zeros((STATS - len(pieces), HD), F32))
    return jnp.concatenate(pieces, 0).astype(BF)


def read_stats(rows, count):
    rows, wide, vectors = rows.astype(F32), BLK // HD, []
    for v in range(count):
        at = v * 3 * wide
        parts = [
            rows[at + i : at + i + 1]
            + rows[at + wide + i : at + wide + i + 1]
            + rows[at + 2 * wide + i : at + 2 * wide + i + 1]
            for i in range(wide)
        ]
        vectors.append(jnp.concatenate(parts, 1))
    return vectors


def attend(plan, noisy, tiles, lists):
    n, per, slots, rows, bh = plan.n, plan.per, plan.ctx, plan.rows, plan.bh
    heads, count, relayed = plan.width // HD, len(tiles), len(tiles) != plan.ctx
    scale = 1.0 / math.sqrt(HD)
    log2e = 1.0 / math.log(2.0)
    side = (2 * rows + STATS, plan.width)

    def body(*refs):
        lists_ref, rows_in, tile_refs = refs[0], refs[1 : 1 + n], refs[1 + n : 1 + n + count]
        rows_out = refs[1 + n + count : 1 + 2 * n + count]
        term_refs = refs[1 + 2 * n + count : 1 + 2 * n + count + slots]
        tiles_in, terms_out = refs[1 + 2 * n + count + slots :]
        me, z = lax.axis_index("ctx"), lax.axis_index("head")
        home = lax.div(z, jnp.int32(per))
        if relayed:
            for i in range(slots // 2):
                which = wanted(plan, lists_ref, me, me ^ (2 * i), z)[1]
                for j in range(bh):

                    @pl.when(which == j)
                    def _():
                        tiles_in[2 * i] = tile_refs[i * bh + j][...]

                tiles_in[2 * i + 1] = tile_refs[-1][i]
        else:
            for s in range(slots):
                tiles_in[s] = tile_refs[s][...]

        def step(h, carry):
            cols = pl.ds(pl.multiple_of(h * HD, HD), HD)
            for b in range(bh):
                part = range(b * per, (b + 1) * per)

                def noisy_block(j):
                    return jnp.concatenate([rows_in[m][j, :, cols] for m in part], 0)

                def put_noisy(j, value):
                    value = value.astype(BF).reshape(per, rows, HD)
                    for p in range(per):
                        rows_out[b * per + p][j * rows : (j + 1) * rows, cols] = value[p]

                def clean_block(slot, kv):
                    return tiles_in[slot, kv, :, :, cols].reshape(BLK, HD)

                def put_clean(slot, kv, value):
                    terms_out[slot, kv, :, :, cols] = value.astype(BF).reshape(per, rows, HD)

                q, k0, v0, g = (noisy_block(j) for j in range(4))
                row = me * bh + (b ^ home)
                keys, values, bias, target = [k0], [v0], [None], []
                for s in range(SEL):
                    entry = lists_ref[row, s]
                    live = entry >= 0
                    slot = jnp.where(live, lax.div(entry, jnp.int32(bh)) ^ me, 0)
                    keys.append(clean_block(slot, 0))
                    values.append(clean_block(slot, 1))
                    bias.append(jnp.where(live, 0.0, MASKED).astype(F32))
                    target.append(jnp.where(live, slot, slots))
                scores = []
                for kt, extra in zip(keys, bias):
                    s = dot(kt, q, 1, 1) * (scale * log2e)
                    scores.append(s if extra is None else s + extra)
                top = functools.reduce(
                    jnp.maximum, [jnp.max(s, axis=0, keepdims=True) for s in scores]
                )
                weights = [jnp.exp2(s - top) for s in scores]
                total = functools.reduce(
                    jnp.add, [jnp.sum(w, axis=0, keepdims=True) for w in weights]
                )
                inverse = 1.0 / total
                log_total = top + jnp.log(total) * log2e
                probs = [w * inverse for w in weights]
                probs_bf = [p.astype(BF) for p in probs]
                out_t = functools.reduce(
                    jnp.add, [dot(vt.T, p, 1, 0) for vt, p in zip(values, probs_bf)]
                )
                out_bf = out_t.astype(BF)
                put_noisy(0, out_bf.T)
                delta = jnp.sum(g.T.astype(F32) * out_bf.astype(F32), axis=0, keepdims=True)
                stats = stat_rows(log_total, delta)
                for p in range(per):
                    rows_out[b * per + p][2 * rows :, cols] = stats
                dq_t = jnp.zeros((HD, BLK), F32)
                for t in range(1 + SEL):
                    ds = (probs[t] * (dot(values[t], g, 1, 1) - delta)).astype(BF)
                    dq_t = dq_t + dot(keys[t].T, ds, 1, 0)
                    if t > 0:
                        put_clean(target[t - 1], 0, dot(ds, q, 1, 0) * scale)
                        put_clean(target[t - 1], 1, dot(probs_bf[t], g, 1, 0))
                put_noisy(1, (dq_t * scale).astype(BF).T)
            return carry

        lax.fori_loop(0, heads, step, 0)
        for s in range(slots):
            term_refs[s][...] = terms_out[s]

    flops = heads * bh * 6 * 2 * BLK * (1 + SEL) * BLK * HD
    result = pl.pallas_call(
        body,
        out_shape=[pltpu.VMEM(side, BF)] * n + [pltpu.VMEM(plan.tile, BF)] * slots,
        in_specs=[SMEM] + [VMEM] * (n + count),
        out_specs=[VMEM] * (n + slots),
        scratch_shapes=[
            pltpu.VMEM((slots,) + plan.tile, BF),
            pltpu.VMEM((slots + 1,) + plan.tile, BF),
        ],
        compiler_params=grant(24),
        cost_estimate=cost(
            2 * (slots * plan.tile_bytes + 4 * bh * BLK * plan.width * 2),
            flops,
            heads * bh * BLK * (1 + SEL) * BLK,
        ),
        name="attend",
    )(lists, *on_chip(noisy), *on_chip(tiles))
    return result[:n], result[n:]


def total_terms(plan, terms, lists):
    n, per, slots, rows, bh = plan.n, plan.per, plan.ctx, plan.rows, plan.bh

    def body(*refs):
        lists_ref, ins, outs = refs[0], refs[1 : 1 + slots], refs[1 + slots :]
        me, z = lax.axis_index("ctx"), lax.axis_index("head")
        asked = [wanted(plan, lists_ref, me ^ s, me, z) for s in range(slots)]
        stripe = math.gcd(rows, 32)

        def step(i, carry):
            at = pl.ds(pl.multiple_of(i * stripe, stripe), stripe)
            for kv in range(2):
                for p in range(per):
                    parts = [ins[s][kv, p, at, :].astype(F32) for s in range(slots)]
                    for j in range(bh):
                        acc = jnp.zeros((stripe, plan.width), F32)
                        for (live, which), part in zip(asked, parts):
                            acc = acc + jnp.where((live > 0) & (which == j), part, 0.0)
                        outs[j * per + p][kv, at, :] = acc.astype(BF)
            return carry

        lax.fori_loop(0, rows // stripe, step, 0)

    shape = (2, rows, plan.width)
    return pl.pallas_call(
        body,
        out_shape=[pltpu.VMEM(shape, BF)] * n,
        in_specs=[SMEM] + [VMEM] * slots,
        out_specs=[VMEM] * n,
        compiler_params=grant(4),
        cost_estimate=cost((slots + bh) * plan.tile_bytes),
        name="total_terms",
    )(lists, *on_chip(terms))


def finish(plan, sides, query, grad, key, value):
    n, per, rows, chunks = plan.n, plan.per, plan.rows, plan.chunks
    flat = [p for chunk in sides for p in chunk]
    heads = plan.width // HD
    scale = 1.0 / math.sqrt(HD)
    log2e = 1.0 / math.log(2.0)

    def body(*refs):
        ins, at = refs[: n * chunks], n * chunks
        q_refs, g_refs = refs[at : at + per], refs[at + per : at + 2 * per]
        k_ref, v_ref = refs[at + 2 * per : at + 2 * per + 2]
        outs = refs[at + 2 * per + 2 : at + 2 * per + 6]
        dk_buf, dv_buf, sem, sem_own = refs[at + 2 * per + 6 :]
        z = lax.axis_index("head")
        moves = [
            pltpu.make_async_copy(
                ins[c * n + m].at[pl.ds(j * rows, rows), :],
                outs[j].at[:, plan.cols(z, m, c)],
                sem.at[c * n + m, j],
            )
            for c in range(chunks)
            for m in range(n)
            for j in range(2)
        ]
        for move in moves:
            move.start()
        for c in range(chunks):
            for m in range(n):
                order = [p ^ (m % per) for p in range(per)]
                start = (z ^ m) * plan.group + c * plan.width
                for h in range(heads):
                    cols = pl.ds(pl.multiple_of(start + h * HD, HD), HD)
                    q = jnp.concatenate([q_refs[p][:, cols] for p in order], 0)
                    g = jnp.concatenate([g_refs[p][:, cols] for p in order], 0)
                    log_total, delta = read_stats(
                        ins[c * n + m][2 * rows :, h * HD : (h + 1) * HD], 2
                    )
                    s = dot(k_ref[:, cols], q, 1, 1) * (scale * log2e)
                    prob = jnp.exp2(s - log_total)
                    ds = prob * (dot(v_ref[:, cols], g, 1, 1) - delta)
                    dk_buf[:, cols] = (dot(ds.astype(BF), q, 1, 0) * scale).astype(BF)
                    dv_buf[:, cols] = dot(prob.astype(BF), g, 1, 0).astype(BF)
        own = [
            pltpu.make_async_copy(dk_buf, outs[2], sem_own.at[0]),
            pltpu.make_async_copy(dv_buf, outs[3], sem_own.at[1]),
        ]
        run_all(own)
        for move in moves:
            move.wait()

    shape = (rows, plan.features)
    return pl.pallas_call(
        body,
        out_shape=[jax.ShapeDtypeStruct(shape, BF)] * 4,
        in_specs=[VMEM] * (len(flat) + 2 * per + 2),
        out_specs=[HBM] * 4,
        scratch_shapes=[
            pltpu.VMEM(shape, BF),
            pltpu.VMEM(shape, BF),
            pltpu.SemaphoreType.DMA((len(flat), 2)),
            pltpu.SemaphoreType.DMA((2,)),
        ],
        compiler_params=grant(6),
        cost_estimate=cost(
            12 * rows * plan.features * 2, 4 * 2 * rows * BLK * plan.features, rows * BLK * 16
        ),
        name="finish",
    )(*on_chip(flat), *on_chip(query), *on_chip(grad), *on_chip([key, value]))


def slot_order(slots):
    return sorted(range(1, slots), key=lambda s: (-bin(s >> 1).count("1"), s >> 1 == 0, s))


def over_head(parts):
    got = {0: parts[0]}
    for m in range(len(parts) - 1, 0, -1):
        got[m] = swap(parts[m], "head", m)
    return [got[m] for m in range(len(parts))]


def over_ctx(parts):
    got = {0: parts[0]}
    for s in slot_order(len(parts)):
        got[s] = swap(parts[s], "ctx", s)
    return [got[s] for s in range(len(parts))]


def shards(query, key, value, kclean, vclean, grad, lists):
    plan = Plan(query.shape[0], query.shape[1], lists.shape[0], CHUNKS)
    chunks = range(plan.chunks)
    clean = [over_head(pack(plan, (kclean, vclean), c)) for c in chunks]
    noisy = [over_head(pack(plan, (query, key, value, grad), c)) for c in chunks]
    tiles = [
        relay(plan, clean[c], lists)
        if c in RELAYED and (plan.ctx, plan.bh) == (8, 2)
        else over_ctx(select(plan, clean[c], lists))
        for c in chunks
    ]
    sides, sums = [], []
    for c in chunks:
        side, terms = attend(plan, noisy[c], tiles[c], lists)
        sides.append(over_head(side))
        terms = over_ctx(terms)
        sums.append(over_head(total_terms(plan, terms, lists)))
    masks = range(plan.per)
    block_q = [query if m == 0 else swap(query, "head", m) for m in masks]
    block_g = [grad if m == 0 else swap(grad, "head", m) for m in masks]
    rows = finish(plan, sides, block_q, block_g, key, value)
    return (*rows, *unpack(plan, sums, 2))


def solution(mesh):
    rows = P(("ctx", "head"), None)
    return jax.shard_map(
        shards,
        mesh=mesh,
        in_specs=(rows,) * 6 + (P(),),
        out_specs=(rows,) * 6,
        check_vma=False,
    )
```
